256 devices in a mesh: beam: 16 (over x, z_hi, core), depth: 16 (over y, z_lo).
Axes of the slice: x: 4, y: 4, z: 8 (z_hi: 2, z_lo: 4; z = z_hi * 4 + z_lo), core: 2. Of those that a mesh axis runs over, the one named last changes fastest.
Arguments:
- concentration: float32 [512, 2048, 256], P('beam', 'depth'), may hold values from 0.25 to 2.5
- entry_intensity: float32 [2048, 256], P('depth'), may hold values from 0.25 to 1.75
- absorb: float32 [256], replicated, may hold values from 0.000390625 to 0.0048828125
- blur_taps: float32 [5], replicated, may hold values from 0.1 to 1
- measured: float32 [512, 256], P('beam'), may hold values from -6 to 6
Outputs:
- descent: float32 [512, 2048, 256], P('beam', 'depth')
- residual: float32 [512, 256], P('beam', 'depth')
The draws below stay inside these ranges and needn't reach their ends.
All inputs are finite; a program needn't handle non-finite values.
Results may differ from the reference program's by a relative error of at most 0.000058.
Values sent between devices are 32-bit elements; how exact they have to be, the bound alone decides.
No kernel may reach another device: no remote copies, remote signals or barrier semaphores. Data moves between devices by JAX's collectives and lax.ppermute only.
A program may use at most 64 MiB of HBM per device.

```python
import math
import jax
import jax.numpy as jnp
from jax import lax

CD = 128
H = 256
TAPS = 5
NB = 512
ND = 2048
N_DEPTH = 16


def shard_levels(key, shape, shards, low, high):
    def one(dim, blocks):
        heights = jax.random.uniform(jax.random.fold_in(jax.random.fold_in(key, 6), dim), (blocks,), jnp.float32, low / len(shards), high / len(shards))
        return jnp.repeat(jnp.exp(heights), shape[dim] // blocks).reshape((-1,) + (1,) * (len(shape) - dim - 1))

    gain = one(*shards[0])
    for cut in shards[1:]:
        gain = gain * one(*cut)
    return gain


def bell_draw(own_key, extent, deviation, most, cuts=(), held_as=jnp.bfloat16):
    values = jax.random.normal(own_key, extent, jnp.float32) * deviation
    if len(cuts) > 0:
        values = shard_levels(own_key, extent, cuts, -0.22, 0.18) * values
    return jnp.clip(values, min=-most, max=most).astype(held_as)


def setup_inputs(seed: int = 0) -> dict:
    arg_keys = jax.random.split(jax.random.key(seed), 6)
    concentration = jnp.clip(jnp.exp(math.log(2.5) - 2.3025851 * jax.random.uniform(arg_keys[0], (NB, ND, H), jnp.float32) ** shard_levels(arg_keys[0], (NB, ND, H), ((0, 16), (1, 16)), -0.2, 0.2)), 0.25, 2.5)
    entry_intensity = jnp.clip(1.0 + 0.15 * jax.random.normal(arg_keys[1], (ND, H), jnp.float32), 0.25, 1.75)
    absorb = jnp.clip(jnp.exp(jax.random.uniform(arg_keys[2], (H,), jnp.float32, math.log(0.000390625), math.log(0.0048828125))), 0.000390625, 0.0048828125)
    blur_taps = jnp.clip(jnp.exp(jax.random.uniform(arg_keys[3], (TAPS,), jnp.float32, math.log(0.1), math.log(1.0))), 0.1, 1.0)
    measured = bell_draw(arg_keys[4], (NB, H), 1.0, 6.0, ((0, 16),), jnp.float32)
    return {"concentration": concentration, "entry_intensity": entry_intensity, "absorb": absorb, "blur_taps": blur_taps, "measured": measured}


def blur_rows(padded, blur_taps, width):
    total = blur_taps[0] * padded[:, 0:width]
    for k in range(1, 5):
        total = total + blur_taps[k] * padded[:, k:k + width]
    return total


def adjoint_rows(padded, blur_taps, width):
    total = blur_taps[0] * padded[:, 4:4 + width]
    for k in range(1, 5):
        total = total + blur_taps[k] * padded[:, 4 - k:4 - k + width]
    return total


def reference(concentration, entry_intensity, absorb, blur_taps, measured):
    starts = jnp.arange(N_DEPTH, dtype=jnp.int32) * CD

    def lit_block(start):
        block = lax.dynamic_slice_in_dim(concentration, start, CD, 1)
        light = lax.dynamic_slice_in_dim(entry_intensity, start, CD, 0)
        inclusive = jnp.cumsum(block, axis=0)
        prior = jnp.concatenate([jnp.zeros((1, CD, H), jnp.float32), inclusive[:-1]], axis=0)
        lit = light[None] * jnp.exp(-absorb * prior)
        return block, lit

    def emit(start):
        block, lit = lit_block(start)
        return jnp.sum(lit * block, axis=1)

    image = jnp.sum(lax.map(emit, starts), axis=0) / ND
    padded = jnp.pad(image, ((0, 0), (2, 2)))
    residual = blur_rows(padded, blur_taps, H) - measured
    back = adjoint_rows(jnp.pad(residual, ((0, 0), (2, 2))), blur_taps, H)

    def gradient(start):
        block, lit = lit_block(start)
        q = back[:, None, :] * lit
        weighted = q * block
        inclusive = jnp.cumsum(weighted[::-1], axis=0)[::-1]
        later = jnp.concatenate([inclusive[1:], jnp.zeros((1, CD, H), jnp.float32)], axis=0)
        return absorb * later - q

    blocks = lax.map(gradient, starts)
    descent = jnp.transpose(blocks, (1, 0, 2, 3)).reshape(NB, ND, H)
    return descent, residual
```

```python
import jax
import jax.numpy as jnp
from jax import lax
from jax.experimental import pallas as pl
from jax.experimental.pallas import tpu as pltpu
from jax.sharding import Mesh
from jax.sharding import PartitionSpec as P

BEAM = ("x", "zh", "core")
DEPTH = ("y", "zl")
LOG2E = 1.4426950408889634
CHUNKS = 8
VM = pl.BlockSpec(memory_space=pltpu.VMEM)
SM = pl.BlockSpec(memory_space=pltpu.SMEM)
ANY = pl.BlockSpec(memory_space=pl.ANY)
F32 = jnp.float32


def xor(count, bits):
    return [(i, i ^ bits) for i in range(count)]


def call(body, outs, in_specs, out_specs, flops, nbytes, exps=0, scratch=()):
    return pl.pallas_call(
        body,
        out_shape=outs,
        in_specs=in_specs,
        out_specs=out_specs,
        scratch_shapes=scratch,
        cost_estimate=pl.CostEstimate(flops=flops, bytes_accessed=nbytes, transcendentals=exps),
        compiler_params=pltpu.CompilerParams(vmem_limit_bytes=24 * 2**20),
    )


def halves(ref, total):
    rows = total.shape[0] // 2
    core = lax.axis_index("core")
    ref[...] = total
    mine = ref[pl.ds(pl.multiple_of(core * rows, 8), rows), :]
    other = ref[pl.ds(pl.multiple_of((1 - core) * rows, 8), rows), :]
    return mine, other


def joined(ref, mine, other):
    rows = mine.shape[0]
    core = lax.axis_index("core")
    ref[pl.ds(pl.multiple_of(core * rows, 8), rows), :] = mine
    ref[pl.ds(pl.multiple_of((1 - core) * rows, 8), rows), :] = other
    return ref[...]


def load_body(c_hbm, c_ref, mine_ref, other_ref, total_ref, sems):
    beam = c_ref.shape[0]
    step = beam // CHUNKS
    copies = []
    for k in range(CHUNKS):
        part = pl.ds(k * step, step)
        copy = pltpu.make_async_copy(c_hbm.at[part], c_ref.at[part], sems.at[k])
        copy.start()
        copies.append(copy)
    total = None
    for k in range(CHUNKS):
        copies[k].wait()
        part = jnp.sum(c_ref[k * step : (k + 1) * step], axis=0)
        total = part if total is None else total + part
    mine_ref[...], other_ref[...] = halves(total_ref, total)


def local_body(c_ref, absorb_ref, light_ref, emit_ref):
    beam, depth, height = c_ref.shape
    rate = jnp.broadcast_to(absorb_ref[...] * (-LOG2E), (8, height))

    @pl.loop(0, depth // 8)
    def _(i):
        rows = pl.ds(pl.multiple_of(i * 8, 8), 8)
        prior = jnp.zeros((8, height), F32)
        for b in range(beam):
            c = c_ref[b, rows, :]
            light = jnp.exp2(rate * prior)
            light_ref[b, rows, :] = light
            emit_ref[b, rows, :] = light * c
            prior = prior + c


def image_body(mine_ref, other_ref, absorb_ref, entry_ref, emit_ref, entered_ref, part_ref, before_ref):
    beam = emit_ref.shape[0]
    before = joined(before_ref, mine_ref[...], other_ref[...])
    entered = entry_ref[...] * jnp.exp2(before * (absorb_ref[...] * (-LOG2E)))
    entered_ref[...] = entered
    for b in range(beam):
        part_ref[b : b + 1, :] = jnp.sum(entered * emit_ref[b], axis=0, keepdims=True)


def shifted(value, by):
    width = value.shape[1]
    column = lax.broadcasted_iota(jnp.int32, value.shape, 1)
    source = column + by
    moved = pltpu.roll(value, (-by) % width, 1)
    return jnp.where((source >= 0) & (source < width), moved, 0.0)


def blurred(value, taps_ref, sign):
    total = taps_ref[2] * value
    for k in (0, 1, 3, 4):
        total = total + taps_ref[k] * shifted(value, sign * (k - 2))
    return total


def adjoint_body(scale, s0, s1, s2, s3, taps_ref, measured_ref, emit_ref, entered_ref,
                 residual_ref, back_ref, mine_ref, other_ref, total_ref):
    beam = emit_ref.shape[0]
    image = (s0[...] + s1[...] + s2[...] + s3[...]) * scale
    residual = blurred(image, taps_ref, 1) - measured_ref[...]
    residual_ref[...] = residual
    back_ref[...] = blurred(residual, taps_ref, -1)
    total = None
    for b in range(beam):
        term = back_ref[b : b + 1, :] * emit_ref[b]
        total = term if total is None else total + term
    mine_ref[...], other_ref[...] = halves(total_ref, total * entered_ref[...])


def partial_body(absorb_ref, back_ref, entered_ref, light_ref, emit_ref, known_ref):
    beam, depth, height = light_ref.shape
    absorb = jnp.broadcast_to(absorb_ref[...], (8, height))

    @pl.loop(0, depth // 8)
    def _(i):
        rows = pl.ds(pl.multiple_of(i * 8, 8), 8)
        later = jnp.zeros((8, height), F32)
        entered = entered_ref[rows, :]
        for b in reversed(range(beam)):
            back = back_ref[b : b + 1, :]
            known_ref[b, rows, :] = entered * (absorb * later - back * light_ref[b, rows, :])
            later = later + back * emit_ref[b, rows, :]


def final_body(mine_ref, other_ref, absorb_ref, known_ref, out_hbm, after_ref, out_ref, sems):
    beam = known_ref.shape[0]
    step = beam // CHUNKS
    after = joined(after_ref, mine_ref[...], other_ref[...]) * absorb_ref[...]
    copies = []
    for k in range(CHUNKS):
        for b in range(k * step, (k + 1) * step):
            out_ref[b] = known_ref[b] + after
        part = pl.ds(k * step, step)
        copy = pltpu.make_async_copy(out_ref.at[part], out_hbm.at[part], sems.at[k])
        copy.start()
        copies.append(copy)
    for copy in copies:
        copy.wait()


def scanned(mine, other, reverse):
    x, zh, core = (lax.axis_index(name) for name in BEAM)
    partner = lax.ppermute(other, "core", xor(2, 1))
    pair = mine + partner
    rows = [lax.ppermute(pair, "x", xor(4, k)) for k in (1, 2, 3)]
    counted = [((x ^ k) > x) if reverse else ((x ^ k) < x) for k in (1, 2, 3)]
    over_x = sum(jnp.where(count, row, 0.0) for count, row in zip(counted, rows))
    first = 1 if reverse else 0
    sent = over_x + jnp.where(zh == first, pair, 0.0)
    base = over_x + lax.ppermute(sent, "zh", xor(2, 1))
    for_me = base + jnp.where(core == first, 0.0, partner)
    for_other = base + jnp.where(core == first, mine, 0.0)
    return for_me, lax.ppermute(for_other, "core", xor(2, 1))


def local(concentration, entry_intensity, absorb, blur_taps, measured):
    beam, depth, height = concentration.shape
    depth_count = lax.axis_size("y") * lax.axis_size("zl")
    scale = 1.0 / (depth * depth_count)
    block = pltpu.VMEM((beam, depth, height), F32)
    plane = jax.ShapeDtypeStruct((depth, height), F32)
    half = jax.ShapeDtypeStruct((depth // 2, height), F32)
    camera = jax.ShapeDtypeStruct((beam, height), F32)
    size = beam * depth * height
    rate = absorb.reshape(1, height)
    scratch_plane = pltpu.VMEM((depth, height), F32)

    cells, mine, other = call(
        load_body, (block, half, half), [ANY], (VM, VM, VM), size, 8 * size,
        scratch=(scratch_plane, pltpu.SemaphoreType.DMA((CHUNKS,))),
    )(concentration)
    light, emit = call(local_body, (block, block), [VM, VM], (VM, VM), 4 * size, 12 * size, size)(cells, rate)
    before_mine, before_other = scanned(mine, other, False)
    entered, part = call(
        image_body, (plane, camera), [VM] * 5, (VM, VM), 2 * size, 4 * size, depth * height, scratch=(scratch_plane,)
    )(before_mine, before_other, rate, entry_intensity, emit)

    over_y = part
    for k in (1, 2, 3):
        over_y = over_y + lax.ppermute(part, "y", xor(4, k))
    sums = [over_y] + [lax.ppermute(over_y, "zl", xor(4, k)) for k in (1, 2, 3)]

    def adjoint(*refs):
        adjoint_body(scale, *refs)

    full_residual, back, mine, other = call(
        adjoint, (camera, camera, half, half), [VM] * 4 + [SM] + [VM] * 3, (VM,) * 4, 2 * size, 4 * size,
        scratch=(scratch_plane,),
    )(*sums, blur_taps, measured, emit, entered)
    known = call(partial_body, block, [VM] * 5, VM, 6 * size, 12 * size)(rate, back, entered, light, emit)
    after_mine, after_other = scanned(mine, other, True)
    descent = call(
        final_body, jax.ShapeDtypeStruct((beam, depth, height), F32), [VM] * 4, ANY, size, 12 * size,
        scratch=(scratch_plane, pltpu.VMEM((beam, depth, height), F32), pltpu.SemaphoreType.DMA((CHUNKS,))),
    )(after_mine, after_other, rate, known)

    width = height // depth_count
    section = (lax.axis_index("y") * lax.axis_size("zl") + lax.axis_index("zl")) * width
    residual = lax.dynamic_slice_in_dim(full_residual, section, width, 1)
    return descent, residual


def solution(mesh):
    finer = Mesh(mesh.devices.reshape(4, 2, 2, 4, 4), BEAM + DEPTH)
    placed = (P(BEAM, DEPTH, None), P(DEPTH, None), P(), P(), P(BEAM, None))
    return jax.shard_map(
        local,
        mesh=finer,
        in_specs=placed,
        out_specs=(P(BEAM, DEPTH, None), P(BEAM, DEPTH)),
        check_vma=False,
    )
```

```python
import jax
import jax.numpy as jnp
from jax import lax
from jax.experimental import pallas as pl
from jax.experimental.pallas import tpu as pltpu
from jax.sharding import Mesh
from jax.sharding import PartitionSpec as P

BEAM = ("x", "zh", "core")
DEPTH = ("y", "zl")
LOG2E = 1.4426950408889634
CHUNKS = 8
VM = pl.BlockSpec(memory_space=pltpu.VMEM)
SM = pl.BlockSpec(memory_space=pltpu.SMEM)
HBM = pl.BlockSpec(memory_space=pltpu.HBM)
F32 = jnp.float32


def xor(count, bits):
    return [(i, i ^ bits) for i in range(count)]


def call(body, outs, in_specs, out_specs, flops, nbytes, exps=0, scratch=()):
    return pl.pallas_call(
        body,
        out_shape=outs,
        in_specs=in_specs,
        out_specs=out_specs,
        scratch_shapes=scratch,
        cost_estimate=pl.CostEstimate(flops=flops, bytes_accessed=nbytes, transcendentals=exps),
        compiler_params=pltpu.CompilerParams(vmem_limit_bytes=8 * 2**20),
    )


def halves(ref, total):
    rows = total.shape[0] // 2
    core = lax.axis_index("core")
    ref[...] = total
    mine = ref[pl.ds(pl.multiple_of(core * rows, 8), rows), :]
    other = ref[pl.ds(pl.multiple_of((1 - core) * rows, 8), rows), :]
    return mine, other


def joined(ref, mine, other):
    rows = mine.shape[0]
    core = lax.axis_index("core")
    ref[pl.ds(pl.multiple_of(core * rows, 8), rows), :] = mine
    ref[pl.ds(pl.multiple_of((1 - core) * rows, 8), rows), :] = other
    return ref[...]


def load_body(c_hbm, c_ref, mine_ref, other_ref, flag_ref, total_ref, sems):
    beam = c_ref.shape[0]
    step = beam // CHUNKS
    copies = []
    for k in range(CHUNKS):
        part = pl.ds(k * step, step)
        copy = pltpu.make_async_copy(c_hbm.at[part], c_ref.at[part], sems.at[k])
        copy.start()
        copies.append(copy)
    x, zh, core = (lax.axis_index(name) for name in BEAM)
    flags = [zh, core] + [((x ^ k) < x).astype(jnp.int32) for k in (1, 2, 3)]
    for k, flag in enumerate(flags):
        flag_ref[k : k + 1, :] = jnp.full((1, flag_ref.shape[1]), flag.astype(F32))
    total = None
    for k in range(CHUNKS):
        copies[k].wait()
        part = jnp.sum(c_ref[k * step : (k + 1) * step], axis=0)
        total = part if total is None else total + part
    mine_ref[...], other_ref[...] = halves(total_ref, total)


def local_body(c_ref, absorb_ref, light_ref, emit_ref):
    beam, depth, height = c_ref.shape
    rate = jnp.broadcast_to(absorb_ref[...] * (-LOG2E), (8, height))

    @pl.loop(0, depth // 8)
    def _(i):
        rows = pl.ds(pl.multiple_of(i * 8, 8), 8)
        prior = jnp.zeros((8, height), F32)
        for b in range(beam):
            c = c_ref[b, rows, :]
            light = jnp.exp2(rate * prior)
            light_ref[b, rows, :] = light
            emit_ref[b, rows, :] = light * c
            prior = prior + c


def image_body(mine_ref, other_ref, absorb_ref, entry_ref, emit_ref, entered_ref, part_ref, before_ref):
    beam = emit_ref.shape[0]
    before = joined(before_ref, mine_ref[...], other_ref[...])
    entered = entry_ref[...] * jnp.exp2(before * (absorb_ref[...] * (-LOG2E)))
    entered_ref[...] = entered
    for b in range(beam):
        part_ref[b : b + 1, :] = jnp.sum(entered * emit_ref[b], axis=0, keepdims=True)


def shifted(value, by):
    width = value.shape[1]
    column = lax.broadcasted_iota(jnp.int32, value.shape, 1)
    source = column + by
    moved = pltpu.roll(value, (-by) % width, 1)
    return jnp.where((source >= 0) & (source < width), moved, 0.0)


def blurred(value, taps_ref, sign):
    total = taps_ref[2] * value
    for k in (0, 1, 3, 4):
        total = total + taps_ref[k] * shifted(value, sign * (k - 2))
    return total


def adjoint_body(scale, s0, s1, s2, s3, taps_ref, measured_ref, emit_ref, entered_ref,
                 residual_ref, back_ref, mine_ref, other_ref, total_ref):
    beam = emit_ref.shape[0]
    image = (s0[...] + s1[...] + s2[...] + s3[...]) * scale
    residual = blurred(image, taps_ref, 1) - measured_ref[...]
    residual_ref[...] = residual
    back_ref[...] = blurred(residual, taps_ref, -1)
    total = None
    for b in range(beam):
        term = back_ref[b : b + 1, :] * emit_ref[b]
        total = term if total is None else total + term
    mine_ref[...], other_ref[...] = halves(total_ref, total * entered_ref[...])


def partial_body(absorb_ref, back_ref, residual_ref, entered_ref, light_ref, emit_ref,
                 known_ref, columns_ref, turned_ref):
    beam, depth, height = light_ref.shape
    width = columns_ref.shape[0]
    section = (lax.axis_index("y") * lax.axis_size("zl") + lax.axis_index("zl")) * width
    turned_ref[...] = residual_ref[...].T
    columns_ref[...] = turned_ref[pl.ds(pl.multiple_of(section, 8), width), :]
    absorb = jnp.broadcast_to(absorb_ref[...], (8, height))

    @pl.loop(0, depth // 8)
    def _(i):
        rows = pl.ds(pl.multiple_of(i * 8, 8), 8)
        later = jnp.zeros((8, height), F32)
        entered = entered_ref[rows, :]
        for b in reversed(range(beam)):
            back = back_ref[b : b + 1, :]
            known_ref[b, rows, :] = entered * (absorb * later - back * light_ref[b, rows, :])
            later = later + back * emit_ref[b, rows, :]


def final_body(mine_ref, other_ref, absorb_ref, known_ref, out_hbm, after_ref, out_ref, sems):
    beam = known_ref.shape[0]
    step = beam // CHUNKS
    after = joined(after_ref, mine_ref[...], other_ref[...]) * absorb_ref[...]
    copies = []
    for k in range(CHUNKS):
        for b in range(k * step, (k + 1) * step):
            out_ref[b] = known_ref[b] + after
        part = pl.ds(k * step, step)
        copy = pltpu.make_async_copy(out_ref.at[part], out_hbm.at[part], sems.at[k])
        copy.start()
        copies.append(copy)
    for copy in copies:
        copy.wait()


def scanned(mine, other, flags, reverse):
    if reverse:
        flags = 1.0 - flags
    late_z, late_core = flags[0:1], flags[1:2]
    partner = lax.ppermute(other, "core", xor(2, 1))
    pair = mine + partner
    rows = [lax.ppermute(pair, "x", xor(4, k)) for k in (1, 2, 3)]
    over_x = flags[2:3] * rows[0] + flags[3:4] * rows[1] + flags[4:5] * rows[2]
    sent = over_x + (1.0 - late_z) * pair
    crossed = lax.ppermute(sent, "zh", xor(2, 1))
    base = over_x + crossed
    for_me = base + late_core * partner
    for_other = base + (1.0 - late_core) * mine
    return for_me, lax.ppermute(for_other, "core", xor(2, 1))


def local(concentration, entry_intensity, absorb, blur_taps, measured):
    beam, depth, height = concentration.shape
    depth_count = lax.axis_size("y") * lax.axis_size("zl")
    scale = 1.0 / (depth * depth_count)
    width = height // depth_count
    block = pltpu.VMEM((beam, depth, height), F32)
    plane = jax.ShapeDtypeStruct((depth, height), F32)
    half = jax.ShapeDtypeStruct((depth // 2, height), F32)
    camera = jax.ShapeDtypeStruct((beam, height), F32)
    size = beam * depth * height
    rate = absorb.reshape(1, height)
    scratch_plane = pltpu.VMEM((depth, height), F32)

    cells, mine, other, flags = call(
        load_body, (block, half, half, jax.ShapeDtypeStruct((8, height), F32)), [HBM], (VM,) * 4, size, 8 * size,
        scratch=(scratch_plane, pltpu.SemaphoreType.DMA((CHUNKS,))),
    )(pltpu.with_memory_space_constraint(concentration, pltpu.HBM))
    light, emit = call(local_body, (block, block), [VM, VM], (VM, VM), 4 * size, 12 * size, size)(cells, rate)
    before_mine, before_other = scanned(mine, other, flags, False)
    entered, part = call(
        image_body, (plane, camera), [VM] * 5, (VM, VM), 2 * size, 4 * size, depth * height, scratch=(scratch_plane,)
    )(before_mine, before_other, rate, entry_intensity, emit)

    over_y = part
    for k in (1, 2, 3):
        over_y = over_y + lax.ppermute(part, "y", xor(4, k))
    sums = [over_y] + [lax.ppermute(over_y, "zl", xor(4, k)) for k in (1, 2, 3)]

    def adjoint(*refs):
        adjoint_body(scale, *refs)

    full_residual, back, mine, other = call(
        adjoint, (camera, camera, half, half), [VM] * 4 + [SM] + [VM] * 3, (VM,) * 4, 2 * size, 4 * size,
        scratch=(scratch_plane,),
    )(*sums, blur_taps, measured, emit, entered)
    known, columns = call(
        partial_body, (block, jax.ShapeDtypeStruct((width, beam), F32)), [VM] * 6, (VM, VM),
        6 * size, 12 * size, scratch=(pltpu.VMEM((height, beam), F32),),
    )(rate, back, full_residual, entered, light, emit)
    after_mine, after_other = scanned(mine, other, flags, True)
    descent = call(
        final_body, jax.ShapeDtypeStruct((beam, depth, height), F32), [VM] * 4, HBM, size, 12 * size,
        scratch=(scratch_plane, pltpu.VMEM((beam, depth, height), F32), pltpu.SemaphoreType.DMA((CHUNKS,))),
    )(after_mine, after_other, rate, known)
    return descent, columns.T


def solution(mesh):
    finer = Mesh(mesh.devices.reshape(4, 2, 2, 4, 4), BEAM + DEPTH)
    placed = (P(BEAM, DEPTH, None), P(DEPTH, None), P(), P(), P(BEAM, None))
    return jax.shard_map(
        local,
        mesh=finer,
        in_specs=placed,
        out_specs=(P(BEAM, DEPTH, None), P(BEAM, DEPTH)),
        check_vma=False,
    )
```

```python
import jax
import jax.numpy as jnp
from jax import lax
from jax.experimental import pallas as pl
from jax.experimental.pallas import tpu as pltpu
from jax.sharding import Mesh
from jax.sharding import PartitionSpec as P

BEAM = ("x", "zh", "core")
DEPTH = ("y", "zl")
LOG2E = 1.4426950408889634
CHUNKS = 8
VM = pl.BlockSpec(memory_space=pltpu.VMEM)
SM = pl.BlockSpec(memory_space=pltpu.SMEM)
HBM = pl.BlockSpec(memory_space=pltpu.HBM)
F32 = jnp.float32


def xor(count, bits):
    return [(i, i ^ bits) for i in range(count)]


def call(body, outs, in_specs, out_specs, flops, nbytes, exps=0, scratch=(), aliases=None):
    return pl.pallas_call(
        body,
        out_shape=outs,
        in_specs=in_specs,
        out_specs=out_specs,
        scratch_shapes=scratch,
        input_output_aliases=aliases or {},
        cost_estimate=pl.CostEstimate(flops=flops, bytes_accessed=nbytes, transcendentals=exps),
        compiler_params=pltpu.CompilerParams(vmem_limit_bytes=8 * 2**20),
    )


def half_rows(own, count):
    core = lax.axis_index("core")
    return pl.ds(pl.multiple_of((core if own else 1 - core) * count, 8), count)


def loaded(own, c_hbm, c_ref, total_ref, sems):
    beam, count, _ = c_ref.shape
    rows = half_rows(own, count)
    step = beam // CHUNKS
    copies = []
    for k in range(CHUNKS):
        part = pl.ds(k * step, step)
        copy = pltpu.make_async_copy(c_hbm.at[part, rows], c_ref.at[part], sems.at[k])
        copy.start()
        copies.append(copy)
    total = None
    for k in range(CHUNKS):
        copies[k].wait()
        part = jnp.sum(c_ref[k * step : (k + 1) * step], axis=0)
        total = part if total is None else total + part
    total_ref[...] = total


def load_other_body(c_hbm, c_ref, total_ref, flag_ref, sems):
    loaded(False, c_hbm, c_ref, total_ref, sems)
    x, zh, core = (lax.axis_index(name) for name in BEAM)
    flags = [zh, core] + [((x ^ k) < x).astype(jnp.int32) for k in (1, 2, 3)]
    for k, flag in enumerate(flags):
        flag_ref[k : k + 1, :] = jnp.full((1, flag_ref.shape[1]), flag.astype(F32))


def load_own_body(c_hbm, c_ref, total_ref, sems):
    loaded(True, c_hbm, c_ref, total_ref, sems)


def local_body(own_ref, other_ref, absorb_ref, light_ref, emit_ref):
    beam, count, height = own_ref.shape
    rate = jnp.broadcast_to(absorb_ref[...] * (-LOG2E), (8, height))
    for half, c_ref in enumerate((own_ref, other_ref)):

        @pl.loop(0, count // 8)
        def _(i, half=half, c_ref=c_ref):
            rows = pl.ds(pl.multiple_of(i * 8, 8), 8)
            prior = jnp.zeros((8, height), F32)
            for b in range(beam):
                c = c_ref[b, rows, :]
                light = jnp.exp2(rate * prior)
                light_ref[half, b, rows, :] = light
                emit_ref[half, b, rows, :] = light * c
                prior = prior + c


def imaged(half, before_ref, absorb_ref, entry_ref, emit_ref, entered_ref, part_ref, earlier_ref=None):
    beam, count = emit_ref.shape[1:3]
    entry = entry_ref[half_rows(half == 0, count), :]
    entered = entry * jnp.exp2(before_ref[...] * (absorb_ref[...] * (-LOG2E)))
    entered_ref[...] = entered
    for b in range(beam):
        row = jnp.sum(entered * emit_ref[half, b], axis=0, keepdims=True)
        part_ref[b : b + 1, :] = row if earlier_ref is None else row + earlier_ref[b : b + 1, :]


def image_own_body(before_ref, absorb_ref, entry_ref, emit_ref, entered_ref, part_ref):
    imaged(0, before_ref, absorb_ref, entry_ref, emit_ref, entered_ref, part_ref)


def image_other_body(before_ref, absorb_ref, entry_ref, emit_ref, earlier_ref, entered_ref, part_ref):
    imaged(1, before_ref, absorb_ref, entry_ref, emit_ref, entered_ref, part_ref, earlier_ref)


def shifted(value, by):
    width = value.shape[1]
    source = lax.broadcasted_iota(jnp.int32, value.shape, 1) + by
    moved = pltpu.roll(value, (-by) % width, 1)
    return jnp.where((source >= 0) & (source < width), moved, 0.0)


def blurred(value, taps_ref, sign):
    terms = [taps_ref[k] * shifted(value, sign * (k - 2)) for k in (0, 1, 3, 4)]
    return (taps_ref[2] * value + (terms[0] + terms[1])) + (terms[2] + terms[3])


def weighed(half, back_ref, emit_ref, entered_ref):
    total = None
    for b in range(emit_ref.shape[1]):
        term = back_ref[b : b + 1, :] * emit_ref[half, b]
        total = term if total is None else total + term
    return total * entered_ref[...]


def adjoint_other_body(scale, s0, s1, s2, s3, taps_ref, measured_ref, emit_ref, entered_ref,
                       residual_ref, back_ref, total_ref):
    image = ((s0[...] + s1[...]) + (s2[...] + s3[...])) * scale
    residual = blurred(image, taps_ref, 1) - measured_ref[...]
    residual_ref[...] = residual
    back_ref[...] = blurred(residual, taps_ref, -1)
    total_ref[...] = weighed(1, back_ref, emit_ref, entered_ref)


def adjoint_own_body(back_ref, emit_ref, entered_ref, total_ref):
    total_ref[...] = weighed(0, back_ref, emit_ref, entered_ref)


def partial_body(absorb_ref, back_ref, residual_ref, own_entered_ref, other_entered_ref, light_ref, emit_ref,
                 known_ref, columns_ref, turned_ref):
    _, beam, count, height = light_ref.shape
    width = columns_ref.shape[0]
    section = (lax.axis_index("y") * lax.axis_size("zl") + lax.axis_index("zl")) * width
    turned_ref[...] = residual_ref[...].T
    columns_ref[...] = turned_ref[pl.ds(pl.multiple_of(section, 8), width), :]
    absorb = jnp.broadcast_to(absorb_ref[...], (8, height))
    for half, entered_ref in enumerate((own_entered_ref, other_entered_ref)):

        @pl.loop(0, count // 8)
        def _(i, half=half, entered_ref=entered_ref):
            rows = pl.ds(pl.multiple_of(i * 8, 8), 8)
            later = jnp.zeros((8, height), F32)
            entered = entered_ref[rows, :]
            for b in reversed(range(beam)):
                back = back_ref[b : b + 1, :]
                known_ref[half, b, rows, :] = entered * (absorb * later - back * light_ref[half, b, rows, :])
                later = later + back * emit_ref[half, b, rows, :]


def written(half, after_ref, absorb_ref, known_ref, out_hbm, out_ref, sems):
    beam, count = known_ref.shape[1:3]
    rows = half_rows(half == 0, count)
    step = beam // CHUNKS
    after = after_ref[...] * absorb_ref[...]
    copies = []
    for k in range(CHUNKS):
        for b in range(k * step, (k + 1) * step):
            out_ref[b] = known_ref[half, b] + after
        part = pl.ds(k * step, step)
        copy = pltpu.make_async_copy(out_ref.at[part], out_hbm.at[part, rows], sems.at[k])
        copy.start()
        copies.append(copy)
    for copy in copies:
        copy.wait()


def final_own_body(after_ref, absorb_ref, known_ref, out_hbm, out_ref, sems):
    written(0, after_ref, absorb_ref, known_ref, out_hbm, out_ref, sems)


def final_other_body(after_ref, absorb_ref, known_ref, begun_hbm, out_hbm, out_ref, sems):
    written(1, after_ref, absorb_ref, known_ref, out_hbm, out_ref, sems)


def scanned(own, partner, flags, reverse):
    if reverse:
        flags = 1.0 - flags
    late_z, late_core = flags[0:1], flags[1:2]
    pair = own + partner
    rows = [lax.ppermute(pair, "x", xor(4, k)) for k in (1, 2, 3)]
    over_x = flags[2:3] * rows[0] + flags[3:4] * rows[1] + flags[4:5] * rows[2]
    sent = over_x + (1.0 - late_z) * pair
    crossed = lax.ppermute(sent, "zh", xor(2, 1))
    base = over_x + crossed
    for_me = base + late_core * partner
    for_other = base + (1.0 - late_core) * own
    return for_me, lax.ppermute(for_other, "core", xor(2, 1))


def local(concentration, entry_intensity, absorb, blur_taps, measured):
    beam, depth, height = concentration.shape
    count = depth // 2
    depth_count = lax.axis_size("y") * lax.axis_size("zl")
    scale = 1.0 / (depth * depth_count)
    width = height // depth_count
    half_block = pltpu.VMEM((beam, count, height), F32)
    blocks = pltpu.VMEM((2, beam, count, height), F32)
    half = jax.ShapeDtypeStruct((count, height), F32)
    camera = jax.ShapeDtypeStruct((beam, height), F32)
    size = beam * depth * height
    rate = absorb.reshape(1, height)
    copied = pltpu.SemaphoreType.DMA((CHUNKS,))
    source = pltpu.with_memory_space_constraint(concentration, pltpu.HBM)

    other_cells, other, flags = call(
        load_other_body, (half_block, half, jax.ShapeDtypeStruct((8, height), F32)), [HBM], (VM,) * 3,
        size // 2, 4 * size, scratch=(copied,),
    )(source)
    partner = lax.ppermute(other, "core", xor(2, 1))
    own_cells, own = call(
        load_own_body, (half_block, half), [HBM], (VM, VM), size // 2, 4 * size, scratch=(copied,)
    )(source)
    light, emit = call(
        local_body, (blocks, blocks), [VM] * 3, (VM, VM), 4 * size, 12 * size, size
    )(own_cells, other_cells, rate)
    before_own, before_other = scanned(own, partner, flags, False)
    own_entered, part = call(
        image_own_body, (half, camera), [VM] * 4, (VM, VM), size, 2 * size, count * height
    )(before_own, rate, entry_intensity, emit)
    other_entered, part = call(
        image_other_body, (half, camera), [VM] * 5, (VM, VM), size, 2 * size, count * height
    )(before_other, rate, entry_intensity, emit, part)

    over_y = part
    for k in (1, 2, 3):
        over_y = over_y + lax.ppermute(part, "y", xor(4, k))
    sums = [over_y] + [lax.ppermute(over_y, "zl", xor(4, k)) for k in (3, 2, 1)]

    def adjoint_other(*refs):
        adjoint_other_body(scale, *refs)

    full_residual, back, other = call(
        adjoint_other, (camera, camera, half), [VM] * 4 + [SM] + [VM] * 3, (VM,) * 3, size, 2 * size
    )(*sums, blur_taps, measured, emit, other_entered)
    partner = lax.ppermute(other, "core", xor(2, 1))
    own = call(adjoint_own_body, half, [VM] * 3, VM, size, 2 * size)(back, emit, own_entered)
    known, columns = call(
        partial_body, (blocks, jax.ShapeDtypeStruct((width, beam), F32)), [VM] * 7, (VM, VM),
        6 * size, 12 * size, scratch=(pltpu.VMEM((height, beam), F32),),
    )(rate, back, full_residual, own_entered, other_entered, light, emit)
    after_own, after_other = scanned(own, partner, flags, True)
    written_scratch = (pltpu.VMEM((beam, count, height), F32), copied)
    whole = jax.ShapeDtypeStruct((beam, depth, height), F32)
    begun = call(
        final_own_body, whole, [VM] * 3, HBM, size // 2, 6 * size, scratch=written_scratch
    )(after_own, rate, known)
    descent = call(
        final_other_body, whole, [VM] * 3 + [HBM], HBM, size // 2, 6 * size, scratch=written_scratch,
        aliases={3: 0},
    )(after_other, rate, known, begun)
    return descent, columns.T


def solution(mesh):
    finer = Mesh(mesh.devices.reshape(4, 2, 2, 4, 4), BEAM + DEPTH)
    placed = (P(BEAM, DEPTH, None), P(DEPTH, None), P(), P(), P(BEAM, None))
    return jax.shard_map(
        local,
        mesh=finer,
        in_specs=placed,
        out_specs=(P(BEAM, DEPTH, None), P(BEAM, DEPTH)),
        check_vma=False,
    )
```

```python
import jax
import jax.numpy as jnp
from jax import lax
from jax.experimental import pallas as pl
from jax.experimental.pallas import tpu as pltpu
from jax.sharding import Mesh
from jax.sharding import PartitionSpec as P

BEAM = ("x", "zh", "core")
DEPTH = ("y", "zl")
LOG2E = 1.4426950408889634
CHUNKS = 8
VM = pl.BlockSpec(memory_space=pltpu.VMEM)
SM = pl.BlockSpec(memory_space=pltpu.SMEM)
HBM = pl.BlockSpec(memory_space=pltpu.HBM)
F32 = jnp.float32


def xor(count, bits):
    return [(i, i ^ bits) for i in range(count)]


def call(body, outs, in_specs, out_specs, flops, nbytes, exps=0, scratch=(), aliases=None):
    return pl.pallas_call(
        body,
        out_shape=outs,
        in_specs=in_specs,
        out_specs=out_specs,
        scratch_shapes=scratch,
        input_output_aliases=aliases or {},
        cost_estimate=pl.CostEstimate(flops=flops, bytes_accessed=nbytes, transcendentals=exps),
        compiler_params=pltpu.CompilerParams(vmem_limit_bytes=8 * 2**20),
    )


def half_rows(own, count):
    core = lax.axis_index("core")
    return pl.ds(pl.multiple_of((core if own else 1 - core) * count, 8), count)


def loaded(own, c_hbm, c_ref, total_ref, sems):
    beam, count, _ = c_ref.shape
    rows = half_rows(own, count)
    step = beam // CHUNKS
    copies = []
    for k in range(CHUNKS):
        part = pl.ds(k * step, step)
        copy = pltpu.make_async_copy(c_hbm.at[part, rows], c_ref.at[part], sems.at[k])
        copy.start()
        copies.append(copy)
    total = None
    for k in range(CHUNKS):
        copies[k].wait()
        part = jnp.sum(c_ref[k * step : (k + 1) * step], axis=0)
        total = part if total is None else total + part
    total_ref[...] = total


def load_other_body(c_hbm, c_ref, total_ref, flag_ref, sems):
    loaded(False, c_hbm, c_ref, total_ref, sems)
    x, zh, core = (lax.axis_index(name) for name in BEAM)
    flags = [zh, core] + [((x ^ k) < x).astype(jnp.int32) for k in (1, 2, 3)]
    for k, flag in enumerate(flags):
        flag_ref[k : k + 1, :] = jnp.full((1, flag_ref.shape[1]), flag.astype(F32))


def load_own_body(c_hbm, c_ref, total_ref, sems):
    loaded(True, c_hbm, c_ref, total_ref, sems)


def local_body(own_ref, other_ref, absorb_ref, light_ref, emit_ref):
    beam, count, height = own_ref.shape
    rate = jnp.broadcast_to(absorb_ref[...] * (-LOG2E), (8, height))
    for half, c_ref in enumerate((own_ref, other_ref)):

        @pl.loop(0, count // 8)
        def _(i, half=half, c_ref=c_ref):
            rows = pl.ds(pl.multiple_of(i * 8, 8), 8)
            prior = jnp.zeros((8, height), F32)
            for b in range(beam):
                c = c_ref[b, rows, :]
                light = jnp.exp2(rate * prior)
                light_ref[half, b, rows, :] = light
                emit_ref[half, b, rows, :] = light * c
                prior = prior + c


def imaged(half, before_ref, absorb_ref, entry_ref, emit_ref, entered_ref, part_ref, earlier_ref=None):
    beam, count = emit_ref.shape[1:3]
    entry = entry_ref[half_rows(half == 0, count), :]
    entered = entry * jnp.exp2(before_ref[...] * (absorb_ref[...] * (-LOG2E)))
    entered_ref[...] = entered
    for b in range(beam):
        row = jnp.sum(entered * emit_ref[half, b], axis=0, keepdims=True)
        part_ref[b : b + 1, :] = row if earlier_ref is None else row + earlier_ref[b : b + 1, :]


def image_own_body(before_ref, absorb_ref, entry_ref, emit_ref, entered_ref, part_ref):
    imaged(0, before_ref, absorb_ref, entry_ref, emit_ref, entered_ref, part_ref)


def image_other_body(before_ref, absorb_ref, entry_ref, emit_ref, earlier_ref, entered_ref, part_ref):
    imaged(1, before_ref, absorb_ref, entry_ref, emit_ref, entered_ref, part_ref, earlier_ref)


def shifted(value, by):
    width = value.shape[1]
    source = lax.broadcasted_iota(jnp.int32, value.shape, 1) + by
    moved = pltpu.roll(value, (-by) % width, 1)
    return jnp.where((source >= 0) & (source < width), moved, 0.0)


def blurred(value, taps_ref, sign):
    terms = [taps_ref[k] * shifted(value, sign * (k - 2)) for k in (0, 1, 3, 4)]
    return (taps_ref[2] * value + (terms[0] + terms[1])) + (terms[2] + terms[3])


def weighed(half, back_ref, emit_ref, entered_ref):
    total = None
    for b in range(emit_ref.shape[1]):
        term = back_ref[b : b + 1, :] * emit_ref[half, b]
        total = term if total is None else total + term
    return total * entered_ref[...]


def adjoint_other_body(scale, s0, s1, s2, s3, taps_ref, measured_ref, emit_ref, entered_ref,
                       residual_ref, back_ref, total_ref):
    image = ((s0[...] + s1[...]) + (s2[...] + s3[...])) * scale
    residual = blurred(image, taps_ref, 1) - measured_ref[...]
    residual_ref[...] = residual
    back_ref[...] = blurred(residual, taps_ref, -1)
    total_ref[...] = weighed(1, back_ref, emit_ref, entered_ref)


def adjoint_own_body(back_ref, emit_ref, entered_ref, total_ref):
    total_ref[...] = weighed(0, back_ref, emit_ref, entered_ref)


def turn_body(residual_ref, columns_ref, turned_ref):
    width = columns_ref.shape[0]
    section = (lax.axis_index("y") * lax.axis_size("zl") + lax.axis_index("zl")) * width
    turned_ref[...] = residual_ref[...].T
    columns_ref[...] = turned_ref[pl.ds(pl.multiple_of(section, 8), width), :]


def partial_body(absorb_ref, back_ref, own_entered_ref, other_entered_ref, light_ref, emit_ref, known_ref):
    _, beam, count, height = light_ref.shape
    absorb = jnp.broadcast_to(absorb_ref[...], (8, height))
    for half, entered_ref in enumerate((own_entered_ref, other_entered_ref)):

        @pl.loop(0, count // 8)
        def _(i, half=half, entered_ref=entered_ref):
            rows = pl.ds(pl.multiple_of(i * 8, 8), 8)
            later = jnp.zeros((8, height), F32)
            entered = entered_ref[rows, :]
            for b in reversed(range(beam)):
                back = back_ref[b : b + 1, :]
                known_ref[half, b, rows, :] = entered * (absorb * later - back * light_ref[half, b, rows, :])
                later = later + back * emit_ref[half, b, rows, :]


def written(half, after_ref, absorb_ref, known_ref, out_hbm, out_ref, sems):
    beam, count = known_ref.shape[1:3]
    rows = half_rows(half == 0, count)
    step = beam // CHUNKS
    after = after_ref[...] * absorb_ref[...]
    copies = []
    for k in range(CHUNKS):
        for b in range(k * step, (k + 1) * step):
            out_ref[b] = known_ref[half, b] + after
        part = pl.ds(k * step, step)
        copy = pltpu.make_async_copy(out_ref.at[part], out_hbm.at[part, rows], sems.at[k])
        copy.start()
        copies.append(copy)
    for copy in copies:
        copy.wait()


def final_own_body(after_ref, absorb_ref, known_ref, out_hbm, out_ref, sems):
    written(0, after_ref, absorb_ref, known_ref, out_hbm, out_ref, sems)


def final_other_body(after_ref, absorb_ref, known_ref, begun_hbm, out_hbm, out_ref, sems):
    written(1, after_ref, absorb_ref, known_ref, out_hbm, out_ref, sems)


def scanned(own, partner, flags, reverse):
    if reverse:
        flags = 1.0 - flags
    late_z, late_core = flags[0:1], flags[1:2]
    pair = own + partner
    crossed = lax.ppermute(pair, "zh", xor(2, 1))
    both = pair + crossed
    rows = [lax.ppermute(both, "x", xor(4, k)) for k in (1, 2, 3)]
    base = flags[2:3] * rows[0] + flags[3:4] * rows[1] + flags[4:5] * rows[2] + late_z * crossed
    for_me = base + late_core * partner
    for_other = base + (1.0 - late_core) * own
    return for_me, lax.ppermute(for_other, "core", xor(2, 1))


def local(concentration, entry_intensity, absorb, blur_taps, measured):
    beam, depth, height = concentration.shape
    count = depth // 2
    depth_count = lax.axis_size("y") * lax.axis_size("zl")
    scale = 1.0 / (depth * depth_count)
    width = height // depth_count
    half_block = pltpu.VMEM((beam, count, height), F32)
    blocks = pltpu.VMEM((2, beam, count, height), F32)
    half = jax.ShapeDtypeStruct((count, height), F32)
    camera = jax.ShapeDtypeStruct((beam, height), F32)
    size = beam * depth * height
    rate = absorb.reshape(1, height)
    copied = pltpu.SemaphoreType.DMA((CHUNKS,))
    source = pltpu.with_memory_space_constraint(concentration, pltpu.HBM)

    other_cells, other, flags = call(
        load_other_body, (half_block, half, jax.ShapeDtypeStruct((8, height), F32)), [HBM], (VM,) * 3,
        size // 2, 4 * size, scratch=(copied,),
    )(source)
    partner = lax.ppermute(other, "core", xor(2, 1))
    own_cells, own = call(
        load_own_body, (half_block, half), [HBM], (VM, VM), size // 2, 4 * size, scratch=(copied,)
    )(source)
    light, emit = call(
        local_body, (blocks, blocks), [VM] * 3, (VM, VM), 4 * size, 12 * size, size
    )(own_cells, other_cells, rate)
    before_own, before_other = scanned(own, partner, flags, False)
    own_entered, part = call(
        image_own_body, (half, camera), [VM] * 4, (VM, VM), size, 2 * size, count * height
    )(before_own, rate, entry_intensity, emit)
    other_entered, part = call(
        image_other_body, (half, camera), [VM] * 5, (VM, VM), size, 2 * size, count * height
    )(before_other, rate, entry_intensity, emit, part)

    over_z = part
    for k in (1, 2, 3):
        over_z = over_z + lax.ppermute(part, "zl", xor(4, k))
    sums = [over_z] + [lax.ppermute(over_z, "y", xor(4, k)) for k in (1, 2, 3)]

    def adjoint_other(*refs):
        adjoint_other_body(scale, *refs)

    full_residual, back, other = call(
        adjoint_other, (camera, camera, half), [VM] * 4 + [SM] + [VM] * 3, (VM,) * 3, size, 2 * size
    )(*sums, blur_taps, measured, emit, other_entered)
    partner = lax.ppermute(other, "core", xor(2, 1))
    own = call(adjoint_own_body, half, [VM] * 3, VM, size, 2 * size)(back, emit, own_entered)
    known = call(partial_body, blocks, [VM] * 6, VM, 6 * size, 12 * size)(
        rate, back, own_entered, other_entered, light, emit
    )
    columns = call(
        turn_body, jax.ShapeDtypeStruct((width, beam), F32), [VM], VM, 32768, 65536,
        scratch=(pltpu.VMEM((height, beam), F32),),
    )(full_residual)
    after_own, after_other = scanned(own, partner, flags, True)
    written_scratch = (pltpu.VMEM((beam, count, height), F32), copied)
    whole = jax.ShapeDtypeStruct((beam, depth, height), F32)
    begun = call(
        final_own_body, whole, [VM] * 3, HBM, size // 2, 6 * size, scratch=written_scratch
    )(after_own, rate, known)
    descent = call(
        final_other_body, whole, [VM] * 3 + [HBM], HBM, size // 2, 6 * size, scratch=written_scratch,
        aliases={3: 0},
    )(after_other, rate, known, begun)
    return descent, columns.T


def solution(mesh):
    finer = Mesh(mesh.devices.reshape(4, 2, 2, 4, 4), BEAM + DEPTH)
    placed = (P(BEAM, DEPTH, None), P(DEPTH, None), P(), P(), P(BEAM, None))
    return jax.shard_map(
        local,
        mesh=finer,
        in_specs=placed,
        out_specs=(P(BEAM, DEPTH, None), P(BEAM, DEPTH)),
        check_vma=False,
    )
```

```python
import jax
import jax.numpy as jnp
from jax import lax
from jax.experimental import pallas as pl
from jax.experimental.pallas import tpu as pltpu
from jax.sharding import Mesh
from jax.sharding import PartitionSpec as P

BEAM = ("x", "zh", "core")
DEPTH = ("y", "zl")
LOG2E = 1.4426950408889634
CHUNKS = 8
VM = pl.BlockSpec(memory_space=pltpu.VMEM)
SM = pl.BlockSpec(memory_space=pltpu.SMEM)
HBM = pl.BlockSpec(memory_space=pltpu.HBM)
F32 = jnp.float32


def xor(count, bits):
    return [(i, i ^ bits) for i in range(count)]


def call(body, outs, in_specs, out_specs, flops, nbytes, exps=0, scratch=(), aliases=None):
    return pl.pallas_call(
        body,
        out_shape=outs,
        in_specs=in_specs,
        out_specs=out_specs,
        scratch_shapes=scratch,
        input_output_aliases=aliases or {},
        cost_estimate=pl.CostEstimate(flops=flops, bytes_accessed=nbytes, transcendentals=exps),
        compiler_params=pltpu.CompilerParams(vmem_limit_bytes=8 * 2**20),
    )


def half_rows(own, count):
    core = lax.axis_index("core")
    return pl.ds(pl.multiple_of((core if own else 1 - core) * count, 8), count)


def loaded(own, c_hbm, c_ref, total_ref, sems):
    beam, count, _ = c_ref.shape
    rows = half_rows(own, count)
    step = beam // CHUNKS
    copies = []
    for k in range(CHUNKS):
        part = pl.ds(k * step, step)
        copy = pltpu.make_async_copy(c_hbm.at[part, rows], c_ref.at[part], sems.at[k])
        copy.start()
        copies.append(copy)
    total = None
    for k in range(CHUNKS):
        copies[k].wait()
        part = jnp.sum(c_ref[k * step : (k + 1) * step], axis=0)
        total = part if total is None else total + part
    total_ref[...] = total


def load_other_body(c_hbm, c_ref, total_ref, flag_ref, sems):
    loaded(False, c_hbm, c_ref, total_ref, sems)
    x, zh, core = (lax.axis_index(name) for name in BEAM)
    flags = [zh, core] + [((x ^ k) < x).astype(jnp.int32) for k in (1, 2, 3)]
    for k, flag in enumerate(flags):
        flag_ref[k : k + 1, :] = jnp.full((1, flag_ref.shape[1]), flag.astype(F32))


def load_own_body(c_hbm, c_ref, total_ref, sems):
    loaded(True, c_hbm, c_ref, total_ref, sems)


def local_body(own_ref, other_ref, absorb_ref, light_ref, emit_ref):
    beam, count, height = own_ref.shape
    rate = jnp.broadcast_to(absorb_ref[...] * (-LOG2E), (8, height))
    for half, c_ref in enumerate((own_ref, other_ref)):

        @pl.loop(0, count // 8)
        def _(i, half=half, c_ref=c_ref):
            rows = pl.ds(pl.multiple_of(i * 8, 8), 8)
            prior = jnp.zeros((8, height), F32)
            for b in range(beam):
                c = c_ref[b, rows, :]
                light = jnp.exp2(rate * prior)
                light_ref[half, b, rows, :] = light
                emit_ref[half, b, rows, :] = light * c
                prior = prior + c


def imaged(half, before_ref, absorb_ref, entry_ref, emit_ref, entered_ref, part_ref, earlier_ref=None):
    beam, count = emit_ref.shape[1:3]
    entry = entry_ref[half_rows(half == 0, count), :]
    entered = entry * jnp.exp2(before_ref[...] * (absorb_ref[...] * (-LOG2E)))
    entered_ref[...] = entered
    for b in range(beam):
        row = jnp.sum(entered * emit_ref[half, b], axis=0, keepdims=True)
        part_ref[b : b + 1, :] = row if earlier_ref is None else row + earlier_ref[b : b + 1, :]


def image_own_body(before_ref, absorb_ref, entry_ref, emit_ref, entered_ref, part_ref):
    imaged(0, before_ref, absorb_ref, entry_ref, emit_ref, entered_ref, part_ref)


def image_other_body(before_ref, absorb_ref, entry_ref, emit_ref, earlier_ref, entered_ref, part_ref):
    imaged(1, before_ref, absorb_ref, entry_ref, emit_ref, entered_ref, part_ref, earlier_ref)


def product(left, right, contracted=0):
    dims = (((1,), (contracted,)), ((), ()))
    return lax.dot_general(left, right, dims, precision=lax.Precision.HIGHEST, preferred_element_type=F32)


def band_body(scale, taps_ref, measured_ref, band_ref, both_ref, target_ref):
    size = band_ref.shape
    offset = lax.broadcasted_iota(jnp.int32, size, 0) - lax.broadcasted_iota(jnp.int32, size, 1)
    band = jnp.zeros(size, F32)
    for k in range(5):
        band = jnp.where(offset == k - 2, taps_ref[k], band)
    band_ref[...] = band * scale
    both_ref[...] = product(band, band, 1) * scale
    target_ref[...] = product(measured_ref[...], band, 1)


def weighed(half, back_ref, emit_ref, entered_ref):
    total = None
    for b in range(emit_ref.shape[1]):
        term = back_ref[b : b + 1, :] * emit_ref[half, b]
        total = term if total is None else total + term
    return total * entered_ref[...]


def adjoint_other_body(s0, s1, s2, s3, both_ref, target_ref, emit_ref, entered_ref, image_ref, back_ref, total_ref):
    image = (s0[...] + s1[...]) + (s2[...] + s3[...])
    image_ref[...] = image
    back_ref[...] = product(image, both_ref[...]) - target_ref[...]
    total_ref[...] = weighed(1, back_ref, emit_ref, entered_ref)


def adjoint_own_body(back_ref, emit_ref, entered_ref, total_ref):
    total_ref[...] = weighed(0, back_ref, emit_ref, entered_ref)


def turn_body(image_ref, band_ref, measured_ref, columns_ref, turned_ref):
    width = columns_ref.shape[0]
    section = (lax.axis_index("y") * lax.axis_size("zl") + lax.axis_index("zl")) * width
    residual = product(image_ref[...], band_ref[...]) - measured_ref[...]
    turned_ref[...] = residual.T
    columns_ref[...] = turned_ref[pl.ds(pl.multiple_of(section, 8), width), :]


def partial_body(absorb_ref, back_ref, own_entered_ref, other_entered_ref, light_ref, emit_ref, known_ref):
    _, beam, count, height = light_ref.shape
    absorb = jnp.broadcast_to(absorb_ref[...], (8, height))
    for half, entered_ref in enumerate((own_entered_ref, other_entered_ref)):

        @pl.loop(0, count // 8)
        def _(i, half=half, entered_ref=entered_ref):
            rows = pl.ds(pl.multiple_of(i * 8, 8), 8)
            later = jnp.zeros((8, height), F32)
            entered = entered_ref[rows, :]
            for b in reversed(range(beam)):
                back = back_ref[b : b + 1, :]
                known_ref[half, b, rows, :] = entered * (absorb * later - back * light_ref[half, b, rows, :])
                later = later + back * emit_ref[half, b, rows, :]


def written(half, after_ref, absorb_ref, known_ref, out_hbm, out_ref, sems):
    beam, count = known_ref.shape[1:3]
    rows = half_rows(half == 0, count)
    step = beam // CHUNKS
    after = after_ref[...] * absorb_ref[...]
    copies = []
    for k in range(CHUNKS):
        for b in range(k * step, (k + 1) * step):
            out_ref[b] = known_ref[half, b] + after
        part = pl.ds(k * step, step)
        copy = pltpu.make_async_copy(out_ref.at[part], out_hbm.at[part, rows], sems.at[k])
        copy.start()
        copies.append(copy)
    for copy in copies:
        copy.wait()


def final_own_body(after_ref, absorb_ref, known_ref, out_hbm, out_ref, sems):
    written(0, after_ref, absorb_ref, known_ref, out_hbm, out_ref, sems)


def final_other_body(after_ref, absorb_ref, known_ref, begun_hbm, out_hbm, out_ref, sems):
    written(1, after_ref, absorb_ref, known_ref, out_hbm, out_ref, sems)


def exchanged(value, axis):
    rows = []
    for k in (1, 2, 3):
        rows.append(lax.ppermute(value, axis, xor(4, k)))
    return rows


def scanned(own, partner, flags, reverse):
    if reverse:
        flags = 1.0 - flags
    late_z, late_core = flags[0:1], flags[1:2]
    pair = own + partner
    crossed = lax.ppermute(pair, "zh", xor(2, 1))
    both = pair + crossed
    rows = exchanged(both, "x")
    base = flags[2:3] * rows[0] + flags[3:4] * rows[1] + flags[4:5] * rows[2] + late_z * crossed
    for_me = base + late_core * partner
    for_other = base + (1.0 - late_core) * own
    return for_me, lax.ppermute(for_other, "core", xor(2, 1))


def local(concentration, entry_intensity, absorb, blur_taps, measured):
    beam, depth, height = concentration.shape
    count = depth // 2
    depth_count = lax.axis_size("y") * lax.axis_size("zl")
    scale = 1.0 / (depth * depth_count)
    width = height // depth_count
    half_block = pltpu.VMEM((beam, count, height), F32)
    blocks = pltpu.VMEM((2, beam, count, height), F32)
    half = jax.ShapeDtypeStruct((count, height), F32)
    camera = jax.ShapeDtypeStruct((beam, height), F32)
    size = beam * depth * height
    rate = absorb.reshape(1, height)
    copied = pltpu.SemaphoreType.DMA((CHUNKS,))
    source = pltpu.with_memory_space_constraint(concentration, pltpu.HBM)

    other_cells, other, flags = call(
        load_other_body, (half_block, half, jax.ShapeDtypeStruct((8, height), F32)), [HBM], (VM,) * 3,
        size // 2, 4 * size, scratch=(copied,),
    )(source)
    partner = lax.ppermute(other, "core", xor(2, 1))
    own_cells, own = call(
        load_own_body, (half_block, half), [HBM], (VM, VM), size // 2, 4 * size, scratch=(copied,)
    )(source)
    light, emit = call(
        local_body, (blocks, blocks), [VM] * 3, (VM, VM), 4 * size, 12 * size, size
    )(own_cells, other_cells, rate)
    square = jax.ShapeDtypeStruct((height, height), F32)

    def bands(*refs):
        band_body(scale, *refs)

    band, both, target = call(bands, (square, square, camera), [SM, VM], (VM,) * 3, 2**24, 2**20)(blur_taps, measured)
    before_own, before_other = scanned(own, partner, flags, False)
    own_entered, part = call(
        image_own_body, (half, camera), [VM] * 4, (VM, VM), size, 2 * size, count * height
    )(before_own, rate, entry_intensity, emit)
    other_entered, part = call(
        image_other_body, (half, camera), [VM] * 5, (VM, VM), size, 2 * size, count * height
    )(before_other, rate, entry_intensity, emit, part)

    rows = exchanged(part, "zl")
    over_z = (part + rows[0]) + (rows[1] + rows[2])
    sums = [over_z] + exchanged(over_z, "y")

    image, back, other = call(
        adjoint_other_body, (camera, camera, half), [VM] * 8, (VM,) * 3, size, 2 * size
    )(*sums, both, target, emit, other_entered)
    partner = lax.ppermute(other, "core", xor(2, 1))
    own = call(adjoint_own_body, half, [VM] * 3, VM, size, 2 * size)(back, emit, own_entered)
    known = call(partial_body, blocks, [VM] * 6, VM, 6 * size, 12 * size)(
        rate, back, own_entered, other_entered, light, emit
    )
    columns = call(
        turn_body, jax.ShapeDtypeStruct((width, beam), F32), [VM] * 3, VM, 32768, 65536,
        scratch=(pltpu.VMEM((height, beam), F32),),
    )(image, band, measured)
    after_own, after_other = scanned(own, partner, flags, True)
    written_scratch = (pltpu.VMEM((beam, count, height), F32), copied)
    whole = jax.ShapeDtypeStruct((beam, depth, height), F32)
    begun = call(
        final_own_body, whole, [VM] * 3, HBM, size // 2, 6 * size, scratch=written_scratch
    )(after_own, rate, known)
    descent = call(
        final_other_body, whole, [VM] * 3 + [HBM], HBM, size // 2, 6 * size, scratch=written_scratch,
        aliases={3: 0},
    )(after_other, rate, known, begun)
    return descent, columns.T


def solution(mesh):
    finer = Mesh(mesh.devices.reshape(4, 2, 2, 4, 4), BEAM + DEPTH)
    placed = (P(BEAM, DEPTH, None), P(DEPTH, None), P(), P(), P(BEAM, None))
    return jax.shard_map(
        local,
        mesh=finer,
        in_specs=placed,
        out_specs=(P(BEAM, DEPTH, None), P(BEAM, DEPTH)),
        check_vma=False,
    )
```
